32 devices in a mesh: dp: 16 (over z, y, x), mp: 2 (over core).
Axes of the slice: x: 2, y: 2, z: 4, core: 2. Of those that a mesh axis runs over, the one named last changes fastest.
Arguments:
- value_grads: bfloat16 [16, 24, 128, 128], P('dp', 'mp'), may hold values from -2 to 2
- key_grads: bfloat16 [16, 2, 16, 128, 128], P('dp', 'mp'), may hold values from -0.75 to 0.75
- owners: int32 [40, 1], P('mp'), may hold values from 0 to 15; in each aligned block of 20 rows (0 to 19, 20 to 39, ...) at most 2 rows name the same one
- weights: float32 [16, 2, 2, 128, 128], P('dp', 'mp'), may hold values from -6 to 6
- left: float32 [16, 2, 2, 128, 128], P('dp', 'mp'), may hold values from -0.25 to 4, as said below
- right: float32 [16, 2, 2, 128, 128], P('dp', 'mp'), may hold values from -0.25 to 4, as said below
- left_root: float32 [16, 2, 2, 128, 128], P('dp', 'mp'), may hold values from -0.25 to 4
- right_root: float32 [16, 2, 2, 128, 128], P('dp', 'mp'), may hold values from -0.25 to 4
- second: float32 [16, 2, 2, 128, 128], P('dp', 'mp'), may hold values from 0.001 to 0.1
Outputs:
- new_weights: float32 [16, 2, 2, 128, 128], P('dp', 'mp')
- new_left: float32 [16, 2, 2, 128, 128], P('dp', 'mp')
- new_right: float32 [16, 2, 2, 128, 128], P('dp', 'mp')
- new_second: float32 [16, 2, 2, 128, 128], P('dp', 'mp')
- new_values: bfloat16 [24, 128, 128], P('mp')
- new_keys: bfloat16 [16, 128, 128], P('mp')
The draws below stay inside these ranges and needn't reach their ends.
Inputs may be any that keep to these rules, and one draw needn't show every extreme that they name: `owners`: within each aligned block of 20 rows (one index of mp) no dp index appears more than 2 times; some appears exactly 2 times. `left`: Symmetric. `right`: Symmetric.
All inputs are finite; a program needn't handle non-finite values.
Results may differ from the reference program's by a relative error of at most 0.0035.
Values may be sent and summed in bfloat16 or wider, within the bound.
A program may use at most 64 MiB of HBM per device.

```python
import math
import jax
import jax.numpy as jnp
import numpy as np
from jax import lax

B = 128
CAP = 2
KEYB = 16
NBM = 12
VBLOCKS = 24
KBM = 8
ALLB = 20
N_DP = 16
N_MP = 2


def symmetric_draw(key):
    first, other = jax.random.split(key)
    shape = (N_DP, N_MP, CAP, B, B)
    raw = jax.random.truncated_normal(first, -4.0, 4.0, shape, jnp.float32)
    offdiag = jnp.clip((raw + jnp.swapaxes(raw, -1, -2)) * (0.35 / math.sqrt(B)), -0.25, 0.25)
    diagonal = jax.random.uniform(other, shape[:-1], jnp.float32, 0.5, 2.0)
    identity = jnp.eye(B, dtype=jnp.float32)
    return offdiag * (1.0 - identity) + identity * diagonal[..., None]


def draw_left(key, part):
    return symmetric_draw(jax.random.fold_in(key, 11))


def draw_right(key, part):
    return symmetric_draw(jax.random.fold_in(key, 23))


def draw_left_root(key, part):
    return symmetric_draw(jax.random.fold_in(key, 37))


def draw_right_root(key, part):
    return symmetric_draw(jax.random.fold_in(key, 41))


def shard_levels(own_key, dims, pieces, least, high):
    gain = 1.0
    for dim, parts in pieces:
        draws = jax.random.uniform(jax.random.fold_in(jax.random.fold_in(own_key, 6), dim), (parts,), jnp.float32, least / len(pieces), high / len(pieces))
        gain = gain * jnp.repeat(jnp.exp(draws), dims[dim] // parts).reshape((-1,) + (1,) * (len(dims) - 1 - dim))
    return gain


def routed_block(stream_key, own, number, rows, number_of, top, limit, lean):
    order = jax.random.permutation(stream_key, number_of)
    heavy_load, common = portions_of(number_of, rows * top, limit, lean, True), portions_of(number_of, rows * top, limit, lean, False)
    places = jnp.arange(number_of)

    def named(lengths, turn):
        used = int((lengths > 0).sum())
        fixed = max(1, used // 4)
        passed = fixed + (places - fixed + turn * (used - fixed)) % max(1, number_of - fixed)
        return jnp.zeros((number_of,), jnp.int32).at[order[jnp.where(places < fixed, places, passed)]].set(jnp.asarray(lengths, jnp.int32))

    lengths = jnp.where(number % 4 == 0, named(heavy_load, number // 4), named(common, number - number // 4 - 1))
    mixed = jax.random.permutation(jax.random.fold_in(own, 3), number_of)
    giver, taker = mixed[0:number_of // 2 * 2:2], mixed[1:number_of // 2 * 2:2]
    room = jnp.minimum(lengths[giver] - 1, limit - lengths[taker]) // 2
    room = jnp.where((giver == order[0]) | (taker == order[0]) | (lengths[taker] == 0), 0, jnp.maximum(room, 0))
    passed = jax.random.randint(jax.random.fold_in(own, 4), (number_of // 2,), 0, 1 << 20) % (room + 1)
    lengths = lengths.at[giver].add(-passed).at[taker].add(passed)
    labels = jnp.searchsorted(jnp.cumsum(lengths), jnp.arange(rows * top), side="right").astype(jnp.int32)
    grid = labels.reshape(top, rows).T
    grid = grid[jax.random.permutation(jax.random.fold_in(own, 1), rows)]
    turn = jax.random.randint(jax.random.fold_in(own, 2), (rows, 1), 0, top)
    return jnp.take_along_axis(grid, (jnp.arange(top)[None, :] + turn) % top, axis=1)


def portions_of(amount, total, most, skew, full):
    loads = [(1 << 20) // math.isqrt(grade ** skew) + 1 for grade in range(1, amount + 1)]
    largest = most if full else min(most, max(-(-total // amount), total * loads[0] // sum(loads)))
    least = 1 if total - largest >= amount - 1 else 0
    given, rest = [largest] + [least] * (amount - 1), total - largest - least * (amount - 1)
    while rest > 0:
        candidates = [i for i in range(1, amount) if given[i] < largest] or [i for i in range(1, amount) if given[i] < most]
        pool, remaining = sum([loads[i] for i in candidates]), rest
        for i in candidates:
            extra = min(most - given[i], max(1, remaining * loads[i] // pool), rest)
            given[i] = given[i] + extra
            rest = rest - extra
    return np.array(given)


def centred(key, dims, width, reach, shards=(), kind=jnp.bfloat16):
    values = jax.random.normal(key, dims, jnp.float32) * width
    if len(shards) > 0:
        values = shard_levels(key, dims, shards, -0.22, 0.18) * values
    return jnp.clip(values, min=-reach, max=reach).astype(kind)


def setup_inputs(seed: int = 0) -> dict:
    splits = jax.random.split(jax.random.key(seed), 10)
    value_grads = centred(splits[0], (N_DP, VBLOCKS, B, B), 0.125, 2.0, ((0, 16), (1, 2)))
    key_grads = centred(splits[1], (N_DP, N_MP, KEYB, B, B), 0.05, 0.75, ((0, 16), (1, 2)))
    owners_keys = jax.random.split(jax.random.fold_in(splits[2], 1), (N_MP * ALLB) // ALLB)
    owners_turns = jax.random.permutation(jax.random.fold_in(splits[2], 3), (N_MP * ALLB) // ALLB)
    owners = jax.vmap(lambda own, number: routed_block(jax.random.fold_in(splits[2], 2), own, number, ALLB, N_DP, 1, CAP, 2))(owners_keys, owners_turns).reshape((N_MP * ALLB, 1))
    weights = centred(splits[3], (N_DP, N_MP, CAP, B, B), 1.0, 6.0, ((0, 16), (1, 2)), jnp.float32)
    left = draw_left(jax.random.fold_in(splits[9], 71), 0)
    right = draw_right(jax.random.fold_in(splits[9], 71), 0)
    left_root = draw_left_root(jax.random.fold_in(splits[9], 71), 0)
    right_root = draw_right_root(jax.random.fold_in(splits[9], 71), 0)
    second = jnp.clip(jnp.exp(math.log(0.1) - 4.6051702 * jax.random.uniform(splits[8], (N_DP, N_MP, CAP, B, B), jnp.float32) ** shard_levels(splits[8], (N_DP, N_MP, CAP, B, B), ((0, 16), (1, 2)), -0.2, 0.2)), 0.001, 0.1)
    return {"value_grads": value_grads, "key_grads": key_grads, "owners": owners, "weights": weights, "left": left, "right": right, "left_root": left_root, "right_root": right_root, "second": second}


STAT_DECAY = 0.95
ADAM_DECAY = 0.95
LEARN_RATE = 0.1
NORM_EPS = 1e-06

def slot_onehot(owner_ids, slot_count):
    position = jnp.arange(owner_ids.shape[0], dtype=jnp.int32)
    same_owner = owner_ids[:, None] == owner_ids[None, :]
    earlier = position[None, :] < position[:, None]
    slot_rank = lax.optimization_barrier(jnp.sum((same_owner & earlier).astype(jnp.int32), axis=1))
    target = owner_ids * CAP + slot_rank
    return (target[:, None] == jnp.arange(slot_count, dtype=jnp.int32)[None, :]).astype(jnp.float32)

def shampoo(gradient, weights, left, right, left_root, right_root, second):
    high = lax.Precision.HIGHEST
    new_left = STAT_DECAY * left + (1.0 - STAT_DECAY) * jnp.einsum('...ij,...kj->...ik', gradient, gradient, precision=high)
    new_right = STAT_DECAY * right + (1.0 - STAT_DECAY) * jnp.einsum('...ji,...jk->...ik', gradient, gradient, precision=high)
    shaped = jnp.einsum('...ij,...jk->...ik', left_root, gradient, precision=high)
    shaped = jnp.einsum('...ij,...jk->...ik', shaped, right_root, precision=high)
    new_second = ADAM_DECAY * second + (1.0 - ADAM_DECAY) * gradient * gradient
    adam_step = gradient / jnp.sqrt(new_second)
    adam_norm = jnp.sqrt(lax.optimization_barrier(jnp.sum(adam_step * adam_step, axis=(-2, -1), keepdims=True)))
    shaped_norm = jnp.sqrt(lax.optimization_barrier(jnp.sum(shaped * shaped, axis=(-2, -1), keepdims=True)))
    graft_scale = adam_norm / (shaped_norm + NORM_EPS)
    new_weights = weights - LEARN_RATE * graft_scale * shaped
    return (new_weights, new_left, new_right, new_second)

def reference(value_grads, key_grads, owners, weights, left, right, left_root, right_root, second):
    high = lax.Precision.HIGHEST
    slot_count = N_DP * CAP
    value_total = lax.optimization_barrier(jnp.sum(value_grads, axis=0, dtype=jnp.float32))
    key_partial = lax.optimization_barrier(jnp.sum(key_grads, axis=1, dtype=jnp.float32)).astype(jnp.bfloat16)
    key_total = lax.optimization_barrier(jnp.sum(key_partial, axis=0, dtype=jnp.float32))
    tables = []
    gathered = []
    for shard in range(N_MP):
        blocks = jnp.concatenate([value_total[shard * NBM:(shard + 1) * NBM], key_total[shard * KBM:(shard + 1) * KBM]], axis=0)
        one_hot = slot_onehot(owners[shard * ALLB:(shard + 1) * ALLB, 0], slot_count)
        tables.append(one_hot)
        placed = jnp.einsum('bj,bxy->jxy', one_hot, blocks, precision=high)
        gathered.append(placed.reshape(N_DP, CAP, B, B))
    gradient = jnp.stack(gathered, axis=1)
    new_weights, new_left, new_right, new_second = shampoo(gradient, weights, left, right, left_root, right_root, second)
    rounded = new_weights.astype(jnp.bfloat16)
    value_list = []
    key_list = []
    for shard in range(N_MP):
        flat_new = rounded[:, shard].reshape(slot_count, B, B).astype(jnp.float32)
        picked = jnp.einsum('bj,jxy->bxy', tables[shard], flat_new, precision=high).astype(jnp.bfloat16)
        value_list.append(picked[:NBM])
        key_list.append(picked[NBM:])
    new_values = jnp.concatenate(value_list, axis=0)
    new_keys = jnp.concatenate(key_list, axis=0)
    return (new_weights, new_left, new_right, new_second, new_values, new_keys)
```

```python
import jax
import jax.numpy as jnp
from jax import lax
from jax.sharding import PartitionSpec as P

STAT_DECAY = 0.95
ADAM_DECAY = 0.95
LEARN_RATE = 0.1
NORM_EPS = 1e-06


def slot_onehot(owner_ids, capacity, slot_count):
    position = jnp.arange(owner_ids.shape[0], dtype=jnp.int32)
    same_owner = owner_ids[:, None] == owner_ids[None, :]
    earlier = position[None, :] < position[:, None]
    slot_rank = jnp.sum((same_owner & earlier).astype(jnp.int32), axis=1)
    target = owner_ids * capacity + slot_rank
    return (target[:, None] == jnp.arange(slot_count, dtype=jnp.int32)[None, :]).astype(
        jnp.bfloat16
    )


def shampoo(gradient, weights, left, right, left_root, right_root, second):
    high = lax.Precision.HIGHEST
    new_left = STAT_DECAY * left + (1.0 - STAT_DECAY) * jnp.einsum(
        "...ij,...kj->...ik", gradient, gradient, precision=high
    )
    new_right = STAT_DECAY * right + (1.0 - STAT_DECAY) * jnp.einsum(
        "...ji,...jk->...ik", gradient, gradient, precision=high
    )
    shaped = jnp.einsum("...ij,...jk->...ik", left_root, gradient, precision=high)
    shaped = jnp.einsum("...ij,...jk->...ik", shaped, right_root, precision=high)
    new_second = ADAM_DECAY * second + (1.0 - ADAM_DECAY) * gradient * gradient
    adam_step = gradient / jnp.sqrt(new_second)
    adam_norm = jnp.sqrt(jnp.sum(adam_step * adam_step, axis=(-2, -1), keepdims=True))
    shaped_norm = jnp.sqrt(jnp.sum(shaped * shaped, axis=(-2, -1), keepdims=True))
    graft_scale = adam_norm / (shaped_norm + NORM_EPS)
    new_weights = weights - LEARN_RATE * graft_scale * shaped
    return (new_weights, new_left, new_right, new_second)


def on_device(value_grads, key_grads, owners, weights, left, right, left_root, right_root, second):
    dp_count = lax.axis_size("dp")
    capacity = weights.shape[2]
    slot_count = dp_count * capacity
    value_count = value_grads.shape[1]
    side = value_grads.shape[2]
    key_part = lax.psum_scatter(
        key_grads.astype(jnp.float32).astype(jnp.bfloat16), "mp", scatter_dimension=2, tiled=True
    ).astype(jnp.float32)
    key_rows = key_part[0, 0].astype(jnp.bfloat16)
    one_hot = slot_onehot(owners[:, 0], capacity, slot_count)
    blocks = jnp.concatenate([value_grads[0], key_rows], axis=0)
    placed = jnp.einsum("bj,bxy->jxy", one_hot, blocks, preferred_element_type=jnp.float32)
    outgoing = placed.astype(jnp.bfloat16).reshape(dp_count, capacity, side, side)
    incoming = lax.all_to_all(outgoing, "dp", split_axis=0, concat_axis=0, tiled=True)
    gradient = jnp.sum(incoming, axis=0, dtype=jnp.float32)
    new_weights, new_left, new_right, new_second = shampoo(
        gradient,
        weights[0, 0],
        left[0, 0],
        right[0, 0],
        left_root[0, 0],
        right_root[0, 0],
        second[0, 0],
    )
    rounded = new_weights.astype(jnp.bfloat16)
    spread = jnp.broadcast_to(rounded[None], (dp_count,) + rounded.shape)
    everyone = lax.all_to_all(spread, "dp", split_axis=0, concat_axis=0, tiled=True)
    everyone = everyone.reshape(slot_count, side, side)
    picked = jnp.einsum(
        "bj,jxy->bxy", one_hot, everyone, preferred_element_type=jnp.float32
    ).astype(jnp.bfloat16)
    return (
        new_weights[None, None],
        new_left[None, None],
        new_right[None, None],
        new_second[None, None],
        picked[:value_count],
        picked[value_count:],
    )


def solution(mesh):
    return jax.shard_map(
        on_device,
        mesh=mesh,
        in_specs=(
            P("dp", "mp", None, None),
            P("dp", "mp", None, None, None),
            P("mp", None),
            P("dp", "mp", None, None, None),
            P("dp", "mp", None, None, None),
            P("dp", "mp", None, None, None),
            P("dp", "mp", None, None, None),
            P("dp", "mp", None, None, None),
            P("dp", "mp", None, None, None),
        ),
        out_specs=(
            P("dp", "mp", None, None, None),
            P("dp", "mp", None, None, None),
            P("dp", "mp", None, None, None),
            P("dp", "mp", None, None, None),
            P("mp", None, None),
            P("mp", None, None),
        ),
        check_vma=False,
    )
```

```python
import jax
import jax.numpy as jnp
from jax import lax
from jax.sharding import PartitionSpec as P

STAT_DECAY = 0.95
ADAM_DECAY = 0.95
LEARN_RATE = 0.1
NORM_EPS = 1e-06


def slot_onehot(owner_ids, capacity, slot_count):
    position = jnp.arange(owner_ids.shape[0], dtype=jnp.int32)
    same_owner = owner_ids[:, None] == owner_ids[None, :]
    earlier = position[None, :] < position[:, None]
    slot_rank = jnp.sum((same_owner & earlier).astype(jnp.int32), axis=1)
    target = owner_ids * capacity + slot_rank
    return (target[:, None] == jnp.arange(slot_count, dtype=jnp.int32)[None, :]).astype(
        jnp.bfloat16
    )


def shampoo(gradient, weights, left, right, left_root, right_root, second):
    high = lax.Precision.HIGHEST
    new_left = STAT_DECAY * left + (1.0 - STAT_DECAY) * jnp.einsum(
        "...ij,...kj->...ik", gradient, gradient, precision=high
    )
    new_right = STAT_DECAY * right + (1.0 - STAT_DECAY) * jnp.einsum(
        "...ji,...jk->...ik", gradient, gradient, precision=high
    )
    shaped = jnp.einsum("...ij,...jk->...ik", left_root, gradient, precision=high)
    shaped = jnp.einsum("...ij,...jk->...ik", shaped, right_root, precision=high)
    new_second = ADAM_DECAY * second + (1.0 - ADAM_DECAY) * gradient * gradient
    adam_step = gradient / jnp.sqrt(new_second)
    adam_norm = jnp.sqrt(jnp.sum(adam_step * adam_step, axis=(-2, -1), keepdims=True))
    shaped_norm = jnp.sqrt(jnp.sum(shaped * shaped, axis=(-2, -1), keepdims=True))
    graft_scale = adam_norm / (shaped_norm + NORM_EPS)
    new_weights = weights - LEARN_RATE * graft_scale * shaped
    return (new_weights, new_left, new_right, new_second)


def on_device(value_grads, key_grads, owners, weights, left, right, left_root, right_root, second):
    dp_count = lax.axis_size("dp")
    capacity = weights.shape[2]
    slot_count = dp_count * capacity
    value_count = value_grads.shape[1]
    side = value_grads.shape[2]
    mp_count = lax.axis_size("mp")
    key_share = key_grads.shape[2] // mp_count
    shares = key_grads[0, 0].reshape(mp_count, key_share, side, side)
    if mp_count == 2:
        mp_index = lax.axis_index("mp")
        mine = lax.dynamic_index_in_dim(shares, mp_index, axis=0, keepdims=False)
        theirs = lax.dynamic_index_in_dim(shares, 1 - mp_index, axis=0, keepdims=False)
        arrived = lax.ppermute(theirs, "mp", perm=[(0, 1), (1, 0)])
        key_sum = mine.astype(jnp.float32) + arrived.astype(jnp.float32)
    else:
        arrived = lax.all_to_all(shares, "mp", split_axis=0, concat_axis=0, tiled=True)
        key_sum = jnp.sum(arrived, axis=0, dtype=jnp.float32)
    key_rows = key_sum.astype(jnp.bfloat16)
    one_hot = slot_onehot(owners[:, 0], capacity, slot_count)
    blocks = jnp.concatenate([value_grads[0], key_rows], axis=0)
    placed = jnp.einsum("bj,bxy->jxy", one_hot, blocks, preferred_element_type=jnp.float32)
    outgoing = placed.astype(jnp.bfloat16).reshape(dp_count, capacity, side, side)
    incoming = lax.all_to_all(outgoing, "dp", split_axis=0, concat_axis=0, tiled=True)
    gradient = jnp.sum(incoming, axis=0, dtype=jnp.float32)
    new_weights, new_left, new_right, new_second = shampoo(
        gradient,
        weights[0, 0],
        left[0, 0],
        right[0, 0],
        left_root[0, 0],
        right_root[0, 0],
        second[0, 0],
    )
    rounded = new_weights.astype(jnp.bfloat16)
    spread = jnp.broadcast_to(rounded[None], (dp_count,) + rounded.shape)
    everyone = lax.all_to_all(spread, "dp", split_axis=0, concat_axis=0, tiled=True)
    everyone = everyone.reshape(slot_count, side, side)
    picked = jnp.einsum(
        "bj,jxy->bxy", one_hot, everyone, preferred_element_type=jnp.float32
    ).astype(jnp.bfloat16)
    return (
        new_weights[None, None],
        new_left[None, None],
        new_right[None, None],
        new_second[None, None],
        picked[:value_count],
        picked[value_count:],
    )


def solution(mesh):
    return jax.shard_map(
        on_device,
        mesh=mesh,
        in_specs=(
            P("dp", "mp", None, None),
            P("dp", "mp", None, None, None),
            P("mp", None),
            P("dp", "mp", None, None, None),
            P("dp", "mp", None, None, None),
            P("dp", "mp", None, None, None),
            P("dp", "mp", None, None, None),
            P("dp", "mp", None, None, None),
            P("dp", "mp", None, None, None),
        ),
        out_specs=(
            P("dp", "mp", None, None, None),
            P("dp", "mp", None, None, None),
            P("dp", "mp", None, None, None),
            P("dp", "mp", None, None, None),
            P("mp", None, None),
            P("mp", None, None),
        ),
        check_vma=False,
    )
```

```python
import jax
import jax.numpy as jnp
from jax import lax
from jax.sharding import PartitionSpec as P

STAT_DECAY = 0.95
ADAM_DECAY = 0.95
LEARN_RATE = 0.1
NORM_EPS = 1e-06


def slot_onehot(owner_ids, capacity, slot_count):
    position = jnp.arange(owner_ids.shape[0], dtype=jnp.int32)
    same_owner = owner_ids[:, None] == owner_ids[None, :]
    earlier = position[None, :] < position[:, None]
    slot_rank = jnp.sum((same_owner & earlier).astype(jnp.int32), axis=1)
    target = owner_ids * capacity + slot_rank
    return (target[:, None] == jnp.arange(slot_count, dtype=jnp.int32)[None, :]).astype(
        jnp.bfloat16
    )


def shampoo(gradient, weights, left, right, left_root, right_root, second):
    high = lax.Precision.HIGHEST
    new_left = STAT_DECAY * left + (1.0 - STAT_DECAY) * jnp.einsum(
        "...ij,...kj->...ik", gradient, gradient, precision=high
    )
    new_right = STAT_DECAY * right + (1.0 - STAT_DECAY) * jnp.einsum(
        "...ji,...jk->...ik", gradient, gradient, precision=high
    )
    shaped = jnp.einsum("...ij,...jk->...ik", left_root, gradient, precision=high)
    shaped = jnp.einsum("...ij,...jk->...ik", shaped, right_root, precision=high)
    new_second = ADAM_DECAY * second + (1.0 - ADAM_DECAY) * gradient * gradient
    adam_step = gradient / jnp.sqrt(new_second)
    adam_norm = jnp.sqrt(jnp.sum(adam_step * adam_step, axis=(-2, -1), keepdims=True))
    shaped_norm = jnp.sqrt(jnp.sum(shaped * shaped, axis=(-2, -1), keepdims=True))
    graft_scale = adam_norm / (shaped_norm + NORM_EPS)
    new_weights = weights - LEARN_RATE * graft_scale * shaped
    return (new_weights, new_left, new_right, new_second)


def on_device(value_grads, key_grads, owners, weights, left, right, left_root, right_root, second):
    dp_count = lax.axis_size("dp")
    capacity = weights.shape[2]
    slot_count = dp_count * capacity
    value_count = value_grads.shape[1]
    side = value_grads.shape[2]
    mp_count = lax.axis_size("mp")
    key_share = key_grads.shape[2] // mp_count
    shares = key_grads[0, 0].reshape(mp_count, key_share, side, side)
    if mp_count == 2:
        mp_index = lax.axis_index("mp")
        mine = lax.dynamic_index_in_dim(shares, mp_index, axis=0, keepdims=False)
        theirs = lax.dynamic_index_in_dim(shares, 1 - mp_index, axis=0, keepdims=False)
        arrived = lax.ppermute(theirs, "mp", perm=[(0, 1), (1, 0)])
        key_sum = mine.astype(jnp.float32) + arrived.astype(jnp.float32)
    else:
        arrived = lax.all_to_all(shares, "mp", split_axis=0, concat_axis=0, tiled=True)
        key_sum = jnp.sum(arrived, axis=0, dtype=jnp.float32)
    key_rows = key_sum.astype(jnp.bfloat16)
    dp_index = lax.axis_index("dp")
    relative = (owners[:, 0] - dp_index) % dp_count
    send_hot = slot_onehot(relative, capacity, slot_count)
    blocks = jnp.concatenate([value_grads[0], key_rows], axis=0)
    placed = jnp.einsum("bj,bxy->jxy", send_hot, blocks, preferred_element_type=jnp.float32)
    outgoing = placed.astype(jnp.bfloat16).reshape(dp_count, capacity, side, side)
    gradient = outgoing[0].astype(jnp.float32)
    for shift in range(1, dp_count):
        perm = [(i, (i + shift) % dp_count) for i in range(dp_count)]
        gradient = gradient + lax.ppermute(outgoing[shift], "dp", perm=perm).astype(jnp.float32)
    new_weights, new_left, new_right, new_second = shampoo(
        gradient,
        weights[0, 0],
        left[0, 0],
        right[0, 0],
        left_root[0, 0],
        right_root[0, 0],
        second[0, 0],
    )
    rounded = new_weights.astype(jnp.bfloat16)
    arrivals = [rounded]
    for shift in range(1, dp_count):
        perm = [(i, (i + shift) % dp_count) for i in range(dp_count)]
        arrivals.append(lax.ppermute(rounded, "dp", perm=perm))
    everyone = jnp.concatenate(arrivals, axis=0)
    back_hot = slot_onehot((dp_index - owners[:, 0]) % dp_count, capacity, slot_count)
    picked = jnp.einsum(
        "bj,jxy->bxy", back_hot, everyone, preferred_element_type=jnp.float32
    ).astype(jnp.bfloat16)
    return (
        new_weights[None, None],
        new_left[None, None],
        new_right[None, None],
        new_second[None, None],
        picked[:value_count],
        picked[value_count:],
    )


def solution(mesh):
    return jax.shard_map(
        on_device,
        mesh=mesh,
        in_specs=(
            P("dp", "mp", None, None),
            P("dp", "mp", None, None, None),
            P("mp", None),
            P("dp", "mp", None, None, None),
            P("dp", "mp", None, None, None),
            P("dp", "mp", None, None, None),
            P("dp", "mp", None, None, None),
            P("dp", "mp", None, None, None),
            P("dp", "mp", None, None, None),
        ),
        out_specs=(
            P("dp", "mp", None, None, None),
            P("dp", "mp", None, None, None),
            P("dp", "mp", None, None, None),
            P("dp", "mp", None, None, None),
            P("mp", None, None),
            P("mp", None, None),
        ),
        check_vma=False,
    )
```

```python
import jax
import jax.numpy as jnp
from jax import lax
from jax.sharding import PartitionSpec as P

STAT_DECAY = 0.95
ADAM_DECAY = 0.95
LEARN_RATE = 0.1
NORM_EPS = 1e-06


def slot_onehot(owner_ids, capacity, slot_count):
    position = jnp.arange(owner_ids.shape[0], dtype=jnp.int32)
    same_owner = owner_ids[:, None] == owner_ids[None, :]
    earlier = position[None, :] < position[:, None]
    slot_rank = jnp.sum((same_owner & earlier).astype(jnp.int32), axis=1)
    target = owner_ids * capacity + slot_rank
    return (target[:, None] == jnp.arange(slot_count, dtype=jnp.int32)[None, :]).astype(
        jnp.bfloat16
    )


def shampoo(gradient, weights, left, right, left_root, right_root, second):
    high = lax.Precision.HIGHEST
    new_left = STAT_DECAY * left + (1.0 - STAT_DECAY) * jnp.einsum(
        "...ij,...kj->...ik", gradient, gradient, precision=high
    )
    new_right = STAT_DECAY * right + (1.0 - STAT_DECAY) * jnp.einsum(
        "...ji,...jk->...ik", gradient, gradient, precision=high
    )
    shaped = jnp.einsum("...ij,...jk->...ik", left_root, gradient, precision=high)
    shaped = jnp.einsum("...ij,...jk->...ik", shaped, right_root, precision=high)
    new_second = ADAM_DECAY * second + (1.0 - ADAM_DECAY) * gradient * gradient
    adam_step = gradient / jnp.sqrt(new_second)
    adam_norm = jnp.sqrt(jnp.sum(adam_step * adam_step, axis=(-2, -1), keepdims=True))
    shaped_norm = jnp.sqrt(jnp.sum(shaped * shaped, axis=(-2, -1), keepdims=True))
    graft_scale = adam_norm / (shaped_norm + NORM_EPS)
    new_weights = weights - LEARN_RATE * graft_scale * shaped
    return (new_weights, new_left, new_right, new_second)


def on_device(value_grads, key_grads, owners, weights, left, right, left_root, right_root, second):
    dp_count = lax.axis_size("dp")
    capacity = weights.shape[2]
    slot_count = dp_count * capacity
    value_count = value_grads.shape[1]
    side = value_grads.shape[2]
    mp_count = lax.axis_size("mp")
    key_share = key_grads.shape[2] // mp_count
    shares = key_grads[0, 0].reshape(mp_count, key_share, side, side)
    if mp_count == 2:
        mp_index = lax.axis_index("mp")
        mine = lax.dynamic_index_in_dim(shares, mp_index, axis=0, keepdims=False)
        theirs = lax.dynamic_index_in_dim(shares, 1 - mp_index, axis=0, keepdims=False)
        arrived = lax.ppermute(theirs, "mp", perm=[(0, 1), (1, 0)])
        key_sum = mine.astype(jnp.float32) + arrived.astype(jnp.float32)
    else:
        arrived = lax.all_to_all(shares, "mp", split_axis=0, concat_axis=0, tiled=True)
        key_sum = jnp.sum(arrived, axis=0, dtype=jnp.float32)
    key_rows = key_sum.astype(jnp.bfloat16)
    dp_index = lax.axis_index("dp")
    relative = (owners[:, 0] - dp_index) % dp_count
    send_hot = slot_onehot(relative, capacity, slot_count)
    blocks = jnp.concatenate([value_grads[0], key_rows], axis=0)
    placed = jnp.einsum("bj,bxy->jxy", send_hot, blocks, preferred_element_type=jnp.float32)
    outgoing = placed.astype(jnp.bfloat16).reshape(dp_count, capacity, side, side)
    gradient = outgoing[0].astype(jnp.float32)
    for shift in range(1, dp_count):
        perm = [(i, (i + shift) % dp_count) for i in range(dp_count)]
        gradient = gradient + lax.ppermute(outgoing[shift], "dp", perm=perm).astype(jnp.float32)
    new_weights, new_left, new_right, new_second = shampoo(
        gradient,
        weights[0, 0],
        left[0, 0],
        right[0, 0],
        left_root[0, 0],
        right_root[0, 0],
        second[0, 0],
    )
    rounded = new_weights.astype(jnp.bfloat16)
    spread = jnp.broadcast_to(rounded[None], (dp_count,) + rounded.shape)
    everyone = lax.all_to_all(spread, "dp", split_axis=0, concat_axis=0, tiled=True)
    everyone = everyone.reshape(slot_count, side, side)
    back_hot = slot_onehot(owners[:, 0], capacity, slot_count)
    picked = jnp.einsum(
        "bj,jxy->bxy", back_hot, everyone, preferred_element_type=jnp.float32
    ).astype(jnp.bfloat16)
    return (
        new_weights[None, None],
        new_left[None, None],
        new_right[None, None],
        new_second[None, None],
        picked[:value_count],
        picked[value_count:],
    )


def solution(mesh):
    return jax.shard_map(
        on_device,
        mesh=mesh,
        in_specs=(
            P("dp", "mp", None, None),
            P("dp", "mp", None, None, None),
            P("mp", None),
            P("dp", "mp", None, None, None),
            P("dp", "mp", None, None, None),
            P("dp", "mp", None, None, None),
            P("dp", "mp", None, None, None),
            P("dp", "mp", None, None, None),
            P("dp", "mp", None, None, None),
        ),
        out_specs=(
            P("dp", "mp", None, None, None),
            P("dp", "mp", None, None, None),
            P("dp", "mp", None, None, None),
            P("dp", "mp", None, None, None),
            P("mp", None, None),
            P("mp", None, None),
        ),
        check_vma=False,
    )
```
